32 devices in a mesh: row: 8 (over y, x, core), col: 4 (over z).
Axes of the slice: x: 2, y: 2, z: 4, core: 2. Of those that a mesh axis runs over, the one named last changes fastest.
Arguments:
- homolog_embedding: bfloat16 [32, 1024, 64], P(('row', 'col')), may hold values from -6 to 6
- split_mapping_matrix: bfloat16 [64, 64], replicated, may hold values from -0.75 to 0.75
- couple_mapping_matrix: bfloat16 [1024, 128], replicated, may hold values from -1.5 to 1.5
- couple_offset_vector: bfloat16 [128], replicated, may hold values from -3 to 3
- incoming_adjoint_couple: bfloat16 [1024, 1024, 128], P('row', 'col'), may hold values from -0.29882812 to 0.29882812
Outputs:
- pair_delta_output: bfloat16 [1024, 1024, 128], P('row', 'col')
- alignment_gradient: bfloat16 [32, 1024, 64], P(('row', 'col'))
- out_weight_grad: float32 [1024, 128], replicated
The draws below stay inside these ranges and needn't reach their ends.
All inputs are finite; a program needn't handle non-finite values.
Results may differ from the reference program's by a relative error of at most 0.015.
Values may be sent and summed in bfloat16 or wider, within the bound.
No kernel may reach another device: no remote copies, remote signals or barrier semaphores. Data moves between devices by JAX's collectives and lax.ppermute only.
A program may use at most 128 MiB of HBM per device.

```python
import jax
import jax.numpy as jnp
from jax import lax

FEATURE_DEPTH = 64
HIDDEN_WIDTH = 32
CZ = 128
CHAIN_LENGTH = 1024
ROW_TOTAL = 32


def level_of(key, extent, cuts, low, largest):
    gain, own = 1.0, jax.random.fold_in(key, 6)
    for dim, shards_of in cuts:
        heights = jnp.exp(jax.random.uniform(jax.random.fold_in(own, dim), (shards_of,), jnp.float32, low / len(cuts), largest / len(cuts)))
        gain = gain * jnp.repeat(heights, extent[dim] // shards_of).reshape([-1 if axis == dim else 1 for axis in range(len(extent))])
    return gain


def centred(own_key, shape, width, bound, split=(), kind=jnp.bfloat16):
    values = width * jax.random.normal(own_key, shape, jnp.float32)
    if split:
        values = values * level_of(own_key, shape, split, -0.22, 0.18)
    return jnp.clip(values, -bound, bound).astype(kind)


def setup_inputs(seed: int = 0) -> dict:
    seeds = jax.random.split(jax.random.key(seed), 6)
    return {
        "homolog_embedding": centred(seeds[0], (ROW_TOTAL, CHAIN_LENGTH, FEATURE_DEPTH), 1.0, 6.0, ((0, 32),)),
        "split_mapping_matrix": centred(seeds[1], (FEATURE_DEPTH, 2 * HIDDEN_WIDTH), FEATURE_DEPTH ** -0.5, 0.75),
        "couple_mapping_matrix": centred(seeds[2], (HIDDEN_WIDTH * HIDDEN_WIDTH, CZ), 0.25, 1.5),
        "couple_offset_vector": centred(seeds[3], (CZ,), 0.5, 3.0),
        "incoming_adjoint_couple": centred(seeds[4], (CHAIN_LENGTH, CHAIN_LENGTH, CZ), 0.05, 0.29882812, ((0, 8), (1, 4))),
    }


def standardize_features(homolog_embedding):
    mapped_halves = homolog_embedding.astype(jnp.float32)
    center = lax.optimization_barrier(jnp.mean(mapped_halves, axis=-1, keepdims=True))
    spread = lax.optimization_barrier(jnp.mean((mapped_halves - center) * (mapped_halves - center), axis=-1, keepdims=True))
    reciprocal_spread = lax.rsqrt(spread + 1e-05)
    return ((mapped_halves - center) * reciprocal_spread, reciprocal_spread)

def reference(homolog_embedding, split_mapping_matrix, couple_mapping_matrix, couple_offset_vector, incoming_adjoint_couple):
    standardized_activations, reciprocal_spread = standardize_features(homolog_embedding)
    normalized_input = standardized_activations.astype(jnp.bfloat16)
    factors = jnp.dot(normalized_input, split_mapping_matrix, preferred_element_type=jnp.float32).astype(jnp.bfloat16)
    left = factors[..., :HIDDEN_WIDTH]
    right = factors[..., HIDDEN_WIDTH:]
    block_rows = min(CHAIN_LENGTH, 64)
    count = CHAIN_LENGTH // block_rows
    left_blocks = left.reshape(ROW_TOTAL, count, block_rows, HIDDEN_WIDTH).transpose(1, 0, 2, 3)
    cot_blocks = incoming_adjoint_couple.reshape(count, block_rows, CHAIN_LENGTH, CZ)
    right_wide = right.astype(jnp.float32)

    def advance(carry, inputs):
        weight_sum, right_sum = carry
        left_block, cot_block = inputs
        left_wide = left_block.astype(jnp.float32)
        outer = jnp.einsum('sic,sje->ijce', left_wide, right_wide) / ROW_TOTAL
        flat = outer.astype(jnp.bfloat16).reshape(block_rows * CHAIN_LENGTH, HIDDEN_WIDTH * HIDDEN_WIDTH)
        update = (jnp.dot(flat, couple_mapping_matrix, preferred_element_type=jnp.float32) + couple_offset_vector.astype(jnp.float32)).astype(jnp.bfloat16)
        grad_rows = cot_block.reshape(block_rows * CHAIN_LENGTH, CZ)
        outer_grad = jnp.dot(grad_rows, couple_mapping_matrix.T, preferred_element_type=jnp.float32).astype(jnp.bfloat16)
        outer_grad = outer_grad.reshape(block_rows, CHAIN_LENGTH, HIDDEN_WIDTH, HIDDEN_WIDTH).astype(jnp.float32)
        weight_sum = weight_sum + jnp.dot(flat.T, grad_rows, preferred_element_type=jnp.float32)
        left_grad = jnp.einsum('ijce,sje->sic', outer_grad, right_wide) / ROW_TOTAL
        right_sum = right_sum + jnp.einsum('ijce,sic->sje', outer_grad, left_wide) / ROW_TOTAL
        return ((weight_sum, right_sum), (update.reshape(block_rows, CHAIN_LENGTH, CZ), left_grad))
    start = (jnp.zeros((HIDDEN_WIDTH * HIDDEN_WIDTH, CZ), jnp.float32), jnp.zeros((ROW_TOTAL, CHAIN_LENGTH, HIDDEN_WIDTH), jnp.float32))
    (factor_weight_gradient, right_grad), (updates, left_grads) = lax.scan(advance, start, (left_blocks, cot_blocks))
    pair_delta_output = updates.reshape(CHAIN_LENGTH, CHAIN_LENGTH, CZ)
    left_grad = left_grads.transpose(1, 0, 2, 3).reshape(ROW_TOTAL, CHAIN_LENGTH, HIDDEN_WIDTH)
    both = jnp.concatenate([left_grad.astype(jnp.bfloat16), right_grad.astype(jnp.bfloat16)], axis=-1)
    normalized_gradient = jnp.dot(both, split_mapping_matrix.T, preferred_element_type=jnp.float32)
    first_factor = lax.optimization_barrier(jnp.mean(normalized_gradient, axis=-1, keepdims=True))
    second_factor = lax.optimization_barrier(jnp.mean(normalized_gradient * standardized_activations, axis=-1, keepdims=True))
    alignment_gradient = (reciprocal_spread * (normalized_gradient - first_factor - standardized_activations * second_factor)).astype(jnp.bfloat16)
    return (pair_delta_output, alignment_gradient, factor_weight_gradient)
```

```python
import functools
import math

import jax
import jax.numpy as jnp
from jax import lax
from jax.experimental import pallas as pl
from jax.experimental.pallas import tpu as pltpu
from jax.sharding import PartitionSpec as P

F32 = jnp.float32
BF16 = jnp.bfloat16
AXES = ("row", "col")
LANES = 128
VMEM_BYTES = 56 << 20
DEPTH = 4
STORED_BYTES = 1 << 25


def dot(a, b, da=1, db=0):
    return lax.dot_general(a, b, (((da,), (db,)), ((), ())), preferred_element_type=F32)


def whole(shape):
    return pl.BlockSpec(shape, lambda *_: (0,) * len(shape))


def call(kernel, grid, ins, outs, scratch, flops, args, aliases={}):
    nbytes = sum(a.size * a.dtype.itemsize for a in args)
    nbytes += sum(math.prod(o.shape) * o.dtype.itemsize for _, o in outs)
    return pl.pallas_call(
        kernel,
        grid_spec=pltpu.PrefetchScalarGridSpec(
            num_scalar_prefetch=0,
            grid=grid,
            in_specs=ins,
            out_specs=[s for s, _ in outs],
            scratch_shapes=scratch,
        ),
        out_shape=[o for _, o in outs],
        input_output_aliases=aliases,
        compiler_params=pltpu.CompilerParams(vmem_limit_bytes=VMEM_BYTES),
        cost_estimate=pl.CostEstimate(flops=flops, bytes_accessed=nbytes, transcendentals=0),
    )(*args)


def normalize(x):
    mu = jnp.mean(x, axis=0, keepdims=True)
    var = jnp.mean((x - mu) * (x - mu), axis=0, keepdims=True)
    rstd = lax.rsqrt(var + 1e-05)
    return (x - mu) * rstd, rstd


def project_kernel(rows, cols, x_ref, w_ref, left_ref, right_ref):
    xhat, _ = normalize(x_ref[0].astype(F32))
    width = w_ref.shape[1] // 2
    part, per_col = left_ref.shape[1], right_ref.shape[2]
    groups = LANES // width
    left = dot(xhat.T.astype(BF16), w_ref[:, :width])
    right = dot(w_ref[:, width:], xhat.astype(BF16), 0, 0).astype(BF16)
    for r in range(rows):
        starts = [(r * groups + k) * part for k in range(groups)]
        packed = jnp.concatenate([left[n : n + part] for n in starts], axis=1).astype(BF16)
        for c in range(cols):
            left_ref[r * cols + c] = packed
            right_ref[r * cols + c] = right[:, c * per_col : (c + 1) * per_col]


def arrange(left_ref, rows_ref, wide_ref):
    seqs, part, _ = left_ref.shape
    for s in range(seqs):
        wide_ref[s * part : (s + 1) * part, :] = left_ref[s].astype(F32)
    for p in range(part):
        block = wide_ref[pl.ds(p, seqs, stride=part), :]
        rows_ref[p * seqs : (p + 1) * seqs, :] = block.astype(BF16)


def unpack(block, width, steps):
    group = pl.program_id(0) // steps
    return pltpu.roll(block.astype(F32), lax.rem(LANES - group * width, LANES), 1)


def t_block(seqs, left, w_ref, t_ref):
    z = t_ref.shape[1] // (left.shape[0] // seqs)
    for e in range(0, w_ref.shape[1] // z, 2):
        o = (dot(left, w_ref[:, e * z : (e + 2) * z]) * (1.0 / seqs)).astype(BF16)
        for k in range(2):
            for i in range(left.shape[0] // seqs):
                t_ref[(e + k) * seqs : (e + k + 1) * seqs, i * z : (i + 1) * z] = o[
                    i * seqs : (i + 1) * seqs, k * z : (k + 1) * z
                ]


def u_block(seqs, rt_ref, g_ref, u_ref):
    step, _, z = g_ref.shape
    for p in range(0, step, 2):
        pair = jnp.concatenate([g_ref[p], g_ref[p + 1]], axis=1)
        for m in range(0, rt_ref.shape[0], 256):
            o = (dot(rt_ref[m : m + 256, :], pair) * (1.0 / seqs)).astype(BF16)
            for k in range(256 // seqs):
                e = m // seqs + k
                for h in range(2):
                    u_ref[(p + h) * seqs : (p + h + 1) * seqs, e * z : (e + 1) * z] = o[
                        k * seqs : (k + 1) * seqs, h * z : (h + 1) * z
                    ]


def pair_block(r_ref, t_ref, bias_ref, out_ref):
    z = out_ref.shape[2]
    for i in range(0, out_ref.shape[0], 2):
        o = dot(r_ref[...], t_ref[:, i * z : (i + 2) * z])
        for h in range(2):
            out_ref[i + h] = (o[:, h * z : (h + 1) * z] + bias_ref[...].astype(F32)).astype(BF16)


def right_block(t_ref, g_ref, acc_ref):
    grads = jnp.concatenate([g_ref[i] for i in range(g_ref.shape[0])], axis=1)
    for m in range(0, t_ref.shape[0], 256):
        o = dot(t_ref[m : m + 256, :], grads, 1, 1)
        for k in range(acc_ref.shape[0]):
            acc_ref[k, m : m + 256, :] += o[:, k * LANES : (k + 1) * LANES]


def right_flush(seqs, acc_ref, out_ref):
    for s in range(seqs):
        for k in range(acc_ref.shape[0]):
            block = acc_ref.at[k][pl.ds(s, out_ref.shape[1], stride=seqs), :]
            out_ref[s, :, k * LANES : (k + 1) * LANES] = block.astype(BF16)


def first():
    return pl.program_id(0) == 0


def last():
    return pl.program_id(0) == pl.num_programs(0) - 1


def step_rows(seqs, step, steps, rows_ref, width):
    size = step * seqs
    start = pl.multiple_of(lax.rem(pl.program_id(0), steps) * size, size)
    return unpack(rows_ref[pl.ds(start, size), :], width, steps)[:, :width].astype(BF16)


def widen(couple_ref, w_ref, wide_ref):
    width = w_ref.shape[0]
    z = couple_ref.shape[1]
    wide_ref[...] = couple_ref[...].astype(F32)
    for e in range(couple_ref.shape[0] // width):
        block = wide_ref[pl.ds(e, width, stride=width), :]
        w_ref[:, e * z : (e + 1) * z] = block.astype(BF16)


def block_in(t_ref, buf_ref, sem, n):
    slot = lax.rem(n, buf_ref.shape[0])
    return pltpu.make_async_copy(t_ref.at[n], buf_ref.at[slot], sem.at[slot])


def block_out(t_ref, buf_ref, sem, n):
    slot = lax.rem(n, buf_ref.shape[0])
    return pltpu.make_async_copy(buf_ref.at[slot], t_ref.at[n], sem.at[slot])


def stream(t_ref, buf_ref, sem):
    i, count, depth = pl.program_id(0), t_ref.shape[0], buf_ref.shape[0]

    @pl.when(first())
    def _():
        for n in range(depth - 1):
            block_in(t_ref, buf_ref, sem, n).start()

    @pl.when(i + depth - 1 < count)
    def _():
        block_in(t_ref, buf_ref, sem, i + depth - 1).start()

    block_in(t_ref, buf_ref, sem, i).wait()
    return buf_ref.at[lax.rem(i, depth)]


def t_kernel(
    seqs, step, steps, left_ref, couple_ref, rows_ref, w_ref, t_ref, wide_ref, tall_ref, buf_ref, sem
):
    i, count, depth = pl.program_id(0), t_ref.shape[0], buf_ref.shape[0]

    @pl.when(first())
    def _():
        arrange(left_ref, rows_ref, wide_ref)
        widen(couple_ref, w_ref, tall_ref)

    @pl.when(i >= depth)
    def _():
        block_out(t_ref, buf_ref, sem, i - depth).wait()

    left = step_rows(seqs, step, steps, rows_ref, w_ref.shape[0])
    t_block(seqs, left, w_ref, buf_ref.at[lax.rem(i, depth)])
    block_out(t_ref, buf_ref, sem, i).start()

    @pl.when(last())
    def _():
        for n in range(count - depth, count):
            block_out(t_ref, buf_ref, sem, n).wait()


def arrange_kernel(left_ref, couple_ref, rows_ref, w_ref, wide_ref, tall_ref):
    arrange(left_ref, rows_ref, wide_ref)
    widen(couple_ref, w_ref, tall_ref)


def arrange_right(all_ref, rt_ref, right_ref, wide_ref):
    seqs, width, jl = all_ref.shape
    for s in range(seqs):
        for k in range(jl // LANES):
            block = all_ref[s, :, k * LANES : (k + 1) * LANES]
            wide_ref[k, s * width : (s + 1) * width, :] = block.astype(F32)
    for e in range(width):
        for k in range(jl // LANES):
            block = wide_ref.at[k][pl.ds(e, seqs, stride=width), :]
            rt_ref[e * seqs : (e + 1) * seqs, k * LANES : (k + 1) * LANES] = block.astype(BF16)
    for n in range(0, width * seqs, LANES):
        right_ref[:, n : n + LANES] = rt_ref[n : n + LANES, :].astype(F32).T.astype(BF16)


def u_kernel(
    seqs, steps, rows_ref, all_ref, g_ref, w_ref, send_ref, right_ref, u_ref, dl_ref, dw_ref, rt_ref, wide_ref
):
    @pl.when(first())
    def _():
        arrange_right(all_ref, rt_ref, right_ref, wide_ref)
        dw_ref[...] = jnp.zeros_like(dw_ref)

    u_block(seqs, rt_ref, g_ref, u_ref)
    size, width, z = u_ref.shape[0], w_ref.shape[0], g_ref.shape[2]
    start = pl.multiple_of(pl.program_id(0) * size, size)
    dl_ref[pl.ds(start, size), :width] = dot(u_ref[...], w_ref[...], 1, 1)
    left_t = unpack(rows_ref[...], width, steps).T[:width].astype(BF16)
    for n in range(0, u_ref.shape[1], 512):
        dw_ref[:, n : n + 512] += dot(left_t, u_ref[:, n : n + 512])

    @pl.when(last())
    def _():
        share = send_ref.shape[1] - width
        per = width // share
        count = dl_ref.shape[0] // seqs
        for d in range(seqs):
            e, c = d // per, d % per * share
            block = dw_ref[c : c + share, e * z : (e + 1) * z]
            send_ref[d, width:, :] = block.astype(BF16)
            block = dl_ref[pl.ds(d, count, stride=seqs), :].T[:width]
            if count < LANES:
                block = jnp.concatenate([block, jnp.zeros((width, LANES - count), F32)], 1)
            send_ref[d, :width, :] = block.astype(BF16)


def right_kernel(seqs, t_ref, g_ref, out_ref, acc_ref, buf_ref, sem):
    block = stream(t_ref, buf_ref, sem)

    @pl.when(first())
    def _():
        acc_ref[...] = jnp.zeros_like(acc_ref)

    right_block(block, g_ref, acc_ref)

    @pl.when(last())
    def _():
        right_flush(seqs, acc_ref, out_ref)


def pair_kernel(r_ref, bias_ref, t_ref, out_ref, buf_ref, sem):
    pair_block(r_ref, stream(t_ref, buf_ref, sem), bias_ref, out_ref)


def fused_kernel(
    seqs, step, steps, rows_ref, w_ref, r_ref, g_ref, bias_ref, pair_out, out_ref, t_ref, acc_ref
):
    @pl.when(first())
    def _():
        acc_ref[...] = jnp.zeros_like(acc_ref)

    left = unpack(rows_ref[...], w_ref.shape[0], steps)[:, : w_ref.shape[0]].astype(BF16)
    t_block(seqs, left, w_ref, t_ref)
    right_block(t_ref, g_ref, acc_ref)
    pair_block(r_ref, t_ref, bias_ref, pair_out)

    @pl.when(last())
    def _():
        right_flush(seqs, acc_ref, out_ref)


def share_kernel(parts_ref, _, out_ref):
    share = parts_ref.shape[1]
    total = parts_ref[0].astype(F32)
    for d in range(1, parts_ref.shape[0]):
        total += parts_ref[d].astype(F32)
    for d in range(out_ref.shape[0]):
        out_ref[d, :share, :] = total.astype(BF16)


def finish_kernel(rows, cols, left_ref, right_ref, x_ref, w_ref, out_ref, weight_ref):
    width = left_ref.shape[1]
    jl = right_ref.shape[2] - LANES
    il = x_ref.shape[2] // rows
    lefts, rights = [], []
    for r in range(rows):
        terms = [left_ref[r * cols + c].astype(F32) for c in range(cols)]
        lefts.append(sum(terms[1:], terms[0])[:, :il])
    for c in range(cols):
        terms = [right_ref[r * cols + c, :, :jl].astype(F32) for r in range(rows)]
        rights.append(sum(terms[1:], terms[0]))
    both = jnp.concatenate([jnp.concatenate(lefts, 1), jnp.concatenate(rights, 1)], 0)
    grad = dot(w_ref[...], both.astype(BF16))
    xhat, rstd = normalize(x_ref[0].astype(F32))
    mean = jnp.mean(grad, axis=0, keepdims=True)
    proj = jnp.mean(grad * xhat, axis=0, keepdims=True)
    out_ref[0] = (rstd * (grad - mean - xhat * proj)).astype(BF16)
    share = width * width // (rows * cols)
    for d in range(rows * cols):
        e, c = d * share // width, d * share % width
        block = right_ref[d, :share, jl:].astype(F32)
        weight_ref[pl.ds(c * width + e, share, stride=width), :] = block


def on_device(x, split, couple, bias, cot):
    rows, cols = lax.axis_size("row"), lax.axis_size("col")
    seqs = rows * cols
    width = split.shape[1] // 2
    length, depth = x.shape[1], x.shape[2]
    il, jl, z = cot.shape
    part = il * width // LANES
    step = max(2, 256 // seqs)
    steps = part // step
    grid = (il // step,)
    shape = jax.ShapeDtypeStruct
    x_t = x.transpose(0, 2, 1)

    left_send, right_send = call(
        functools.partial(project_kernel, rows, cols),
        (1,),
        [whole(x_t.shape), whole(split.shape)],
        [
            (whole((seqs, part, LANES)), shape((seqs, part, LANES), BF16)),
            (whole((seqs, width, jl)), shape((seqs, width, jl), BF16)),
        ],
        [],
        2 * length * depth * depth,
        (x_t, split),
    )
    left_all = lax.all_to_all(left_send, AXES, 0, 0, tiled=True)
    right_all = lax.all_to_all(right_send, AXES, 0, 0, tiled=True)
    bias_row = bias[None, :]

    unit = 2 * il * jl * z * seqs * width
    small = 2 * il * seqs * width * width * z
    rows_spec = pl.BlockSpec((step * seqs, LANES), lambda i: (lax.rem(i, steps), 0))
    cot_spec = pl.BlockSpec((step, jl, z), lambda i: (i, 0, 0))
    arranged = [
        (whole((part * seqs, LANES)), shape((part * seqs, LANES), BF16)),
        (whole((width, width * z)), shape((width, width * z), BF16)),
    ]
    wides = [pltpu.VMEM((part * seqs, LANES), F32), pltpu.VMEM(couple.shape, F32)]
    t_shape = (il // step, width * seqs, step * z)
    depth = min(DEPTH, t_shape[0])
    any_spec = pl.BlockSpec(memory_space=pl.ANY)
    slots = [pltpu.VMEM((depth, *t_shape[1:]), BF16), pltpu.SemaphoreType.DMA((depth,))]
    stored = 2 * math.prod(t_shape) <= STORED_BYTES
    if stored:
        left_rows, weight, t_all = call(
            functools.partial(t_kernel, seqs, step, steps),
            grid,
            [whole(left_all.shape), whole(couple.shape)],
            arranged + [(any_spec, shape(t_shape, BF16))],
            wides + slots,
            small,
            (left_all, couple),
        )
        right_all, t_all = lax.optimization_barrier((right_all, t_all))
    else:
        left_rows, weight = call(
            arrange_kernel,
            (1,),
            [whole(left_all.shape), whole(couple.shape)],
            arranged,
            wides,
            0,
            (left_all, couple),
        )
    share = width * width // seqs
    right_shape = (jl, width * seqs)
    send_one, right = call(
        functools.partial(u_kernel, seqs, steps),
        grid,
        [rows_spec, whole(right_all.shape), cot_spec, whole(weight.shape)],
        [
            (
                whole((seqs, width + share, LANES)),
                shape((seqs, width + share, LANES), BF16),
            ),
            (whole(right_shape), shape(right_shape, BF16)),
        ],
        [
            pltpu.VMEM((step * seqs, width * z), BF16),
            pltpu.VMEM((il * seqs, LANES), F32),
            pltpu.VMEM((width, width * z), F32),
            pltpu.VMEM((width * seqs, jl), BF16),
            pltpu.VMEM((jl // LANES, width * seqs, LANES), F32),
        ],
        unit + 2 * small,
        (left_rows, right_all, cot, weight),
    )
    got_one = lax.all_to_all(send_one, AXES, 0, 0, tiled=True)
    right_out = (whole((seqs, width, jl)), shape((seqs, width, jl + LANES), BF16))
    acc = pltpu.VMEM((jl // LANES, width * seqs, LANES), F32)
    if stored:
        (right_back,) = call(
            functools.partial(right_kernel, seqs),
            grid,
            [any_spec, cot_spec],
            [right_out],
            [acc] + slots,
            unit,
            (t_all, cot),
        )
        (pair,) = call(
            pair_kernel,
            grid,
            [whole(right.shape), whole(bias_row.shape), any_spec],
            [(cot_spec, shape(cot.shape, BF16))],
            slots,
            unit,
            (right, bias_row, t_all),
        )
    else:
        pair, right_back = call(
            functools.partial(fused_kernel, seqs, step, steps),
            grid,
            [rows_spec, whole(weight.shape), whole(right.shape), cot_spec, whole(bias_row.shape)],
            [(cot_spec, shape(cot.shape, BF16)), right_out],
            [pltpu.VMEM((width * seqs, step * z), BF16), acc],
            2 * unit + small,
            (left_rows, weight, right, cot, bias_row),
        )
    (send_two,) = call(
        share_kernel,
        (1,),
        [
            pl.BlockSpec((seqs, share, LANES), lambda i: (0, width // share, 0)),
            pl.BlockSpec(memory_space=pl.ANY),
        ],
        [
            (
                pl.BlockSpec((seqs, width, LANES), lambda i: (0, 0, jl // LANES)),
                shape(right_back.shape, BF16),
            )
        ],
        [],
        0,
        (got_one, right_back),
        {1: 0},
    )
    got_two = lax.all_to_all(send_two, AXES, 0, 0, tiled=True)
    align, weight_grad = call(
        functools.partial(finish_kernel, rows, cols),
        (1,),
        [
            pl.BlockSpec((seqs, width, LANES), lambda i: (0, 0, 0)),
            whole(got_two.shape),
            whole(x_t.shape),
            whole(split.shape),
        ],
        [
            (whole(x_t.shape), shape(x_t.shape, BF16)),
            (whole((width * width, z)), shape((width * width, z), F32)),
        ],
        [],
        2 * length * depth * depth,
        (got_one, got_two, x_t, split),
    )
    return pair, align.transpose(0, 2, 1), weight_grad


def solution(mesh):
    placed = (P(AXES, None, None), P(), P(), P(), P("row", "col", None))
    return jax.shard_map(
        on_device,
        mesh=mesh,
        in_specs=placed,
        out_specs=(P("row", "col", None), P(AXES, None, None), P()),
        check_vma=False,
    )
```

```python
import functools
import math

import jax
import jax.numpy as jnp
from jax import lax
from jax.experimental import pallas as pl
from jax.experimental.pallas import tpu as pltpu
from jax.sharding import PartitionSpec as P

F32 = jnp.float32
BF16 = jnp.bfloat16
AXES = ("row", "col")
LANES = 128
VMEM_BYTES = 56 << 20
DEPTH = 3
SMALL_BYTES = 24 << 20
U_BYTES = 48 << 20
STORED_BYTES = 1 << 25


def dot(a, b, da=1, db=0):
    return lax.dot_general(a, b, (((da,), (db,)), ((), ())), preferred_element_type=F32)


def whole(shape):
    return pl.BlockSpec(shape, lambda *_: (0,) * len(shape))


def in_hbm(a):
    return pltpu.with_memory_space_constraint(a, pltpu.HBM)


def call(kernel, grid, ins, outs, scratch, flops, args, aliases={}, limit=VMEM_BYTES):
    nbytes = sum(a.size * a.dtype.itemsize for a in args)
    nbytes += sum(math.prod(o.shape) * o.dtype.itemsize for _, o in outs)
    return pl.pallas_call(
        kernel,
        grid_spec=pltpu.PrefetchScalarGridSpec(
            num_scalar_prefetch=0,
            grid=grid,
            in_specs=ins,
            out_specs=[s for s, _ in outs],
            scratch_shapes=scratch,
        ),
        out_shape=[o for _, o in outs],
        input_output_aliases=aliases,
        compiler_params=pltpu.CompilerParams(vmem_limit_bytes=limit),
        cost_estimate=pl.CostEstimate(flops=flops, bytes_accessed=nbytes, transcendentals=0),
    )(*args)


def normalize(x):
    mu = jnp.mean(x, axis=0, keepdims=True)
    var = jnp.mean((x - mu) * (x - mu), axis=0, keepdims=True)
    rstd = lax.rsqrt(var + 1e-05)
    return (x - mu) * rstd, rstd


def project_kernel(rows, cols, x_ref, w_ref, left_ref, right_ref):
    xhat, _ = normalize(x_ref[0].astype(F32))
    width = w_ref.shape[1] // 2
    part, per_col = left_ref.shape[1], right_ref.shape[2]
    groups = LANES // width
    left = dot(xhat.T.astype(BF16), w_ref[:, :width])
    right = dot(w_ref[:, width:], xhat.astype(BF16), 0, 0).astype(BF16)
    for r in range(rows):
        starts = [(r * groups + k) * part for k in range(groups)]
        packed = jnp.concatenate([left[n : n + part] for n in starts], axis=1).astype(BF16)
        for c in range(cols):
            left_ref[r * cols + c] = packed
            right_ref[r * cols + c] = right[:, c * per_col : (c + 1) * per_col]


def arrange(left_ref, rows_ref, wide_ref):
    seqs, part, _ = left_ref.shape
    for s in range(seqs):
        wide_ref[s * part : (s + 1) * part, :] = left_ref[s].astype(F32)
    for p in range(part):
        block = wide_ref[pl.ds(p, seqs, stride=part), :]
        rows_ref[p * seqs : (p + 1) * seqs, :] = block.astype(BF16)


def unpack(block, width, steps):
    group = pl.program_id(0) // steps
    return pltpu.roll(block.astype(F32), lax.rem(LANES - group * width, LANES), 1)


def t_block(seqs, left, w_ref, t_ref):
    z = t_ref.shape[1] // (left.shape[0] // seqs)
    for e in range(0, w_ref.shape[1] // z, 2):
        o = (dot(left, w_ref[:, e * z : (e + 2) * z]) * (1.0 / seqs)).astype(BF16)
        for k in range(2):
            for i in range(left.shape[0] // seqs):
                t_ref[(e + k) * seqs : (e + k + 1) * seqs, i * z : (i + 1) * z] = o[
                    i * seqs : (i + 1) * seqs, k * z : (k + 1) * z
                ]


def u_block(seqs, rt_ref, g_ref, u_ref):
    step, _, z = g_ref.shape
    for p in range(0, step, 2):
        pair = jnp.concatenate([g_ref[p], g_ref[p + 1]], axis=1)
        for m in range(0, rt_ref.shape[0], 256):
            o = (dot(rt_ref[m : m + 256, :], pair) * (1.0 / seqs)).astype(BF16)
            for k in range(256 // seqs):
                e = m // seqs + k
                for h in range(2):
                    u_ref[(p + h) * seqs : (p + h + 1) * seqs, e * z : (e + 1) * z] = o[
                        k * seqs : (k + 1) * seqs, h * z : (h + 1) * z
                    ]


def pair_block(r_ref, t_ref, bias_ref, out_ref):
    z = out_ref.shape[2]
    for i in range(0, out_ref.shape[0], 2):
        o = dot(r_ref[...], t_ref[:, i * z : (i + 2) * z])
        for h in range(2):
            out_ref[i + h] = (o[:, h * z : (h + 1) * z] + bias_ref[...].astype(F32)).astype(BF16)


def right_block(t_ref, g_ref, acc_ref):
    grads = jnp.concatenate([g_ref[i] for i in range(g_ref.shape[0])], axis=1)
    for m in range(0, t_ref.shape[0], 256):
        o = dot(t_ref[m : m + 256, :], grads, 1, 1)
        for k in range(acc_ref.shape[0]):
            acc_ref[k, m : m + 256, :] += o[:, k * LANES : (k + 1) * LANES]


def right_flush(seqs, acc_ref, out_ref):
    for s in range(seqs):
        for k in range(acc_ref.shape[0]):
            block = acc_ref.at[k][pl.ds(s, out_ref.shape[1], stride=seqs), :]
            out_ref[s, :, k * LANES : (k + 1) * LANES] = block.astype(BF16)


def first():
    return pl.program_id(0) == 0


def last():
    return pl.program_id(0) == pl.num_programs(0) - 1


def step_rows(seqs, step, steps, rows_ref, width):
    size = step * seqs
    start = pl.multiple_of(lax.rem(pl.program_id(0), steps) * size, size)
    return unpack(rows_ref[pl.ds(start, size), :], width, steps)[:, :width].astype(BF16)


def widen(couple_ref, w_ref, wide_ref):
    width = w_ref.shape[0]
    z = couple_ref.shape[1]
    wide_ref[...] = couple_ref[...].astype(F32)
    for e in range(couple_ref.shape[0] // width):
        block = wide_ref[pl.ds(e, width, stride=width), :]
        w_ref[:, e * z : (e + 1) * z] = block.astype(BF16)


def block_in(t_ref, buf_ref, sem, n):
    slot = lax.rem(n, buf_ref.shape[0])
    return pltpu.make_async_copy(t_ref.at[n], buf_ref.at[slot], sem.at[slot])


def block_out(t_ref, buf_ref, sem, n):
    slot = lax.rem(n, buf_ref.shape[0])
    return pltpu.make_async_copy(buf_ref.at[slot], t_ref.at[n], sem.at[slot])


def stream(t_ref, buf_ref, sem):
    i, count, depth = pl.program_id(0), t_ref.shape[0], buf_ref.shape[0]

    @pl.when(first())
    def _():
        for n in range(depth - 1):
            block_in(t_ref, buf_ref, sem, n).start()

    @pl.when(i + depth - 1 < count)
    def _():
        block_in(t_ref, buf_ref, sem, i + depth - 1).start()

    block_in(t_ref, buf_ref, sem, i).wait()
    return buf_ref.at[lax.rem(i, depth)]


def t_kernel(
    seqs, step, steps, left_ref, couple_ref, rows_ref, w_ref, t_ref, wide_ref, tall_ref, buf_ref, sem
):
    i, count, depth = pl.program_id(0), t_ref.shape[0], buf_ref.shape[0]

    @pl.when(first())
    def _():
        arrange(left_ref, rows_ref, wide_ref)
        widen(couple_ref, w_ref, tall_ref)

    @pl.when(i >= depth)
    def _():
        block_out(t_ref, buf_ref, sem, i - depth).wait()

    left = step_rows(seqs, step, steps, rows_ref, w_ref.shape[0])
    t_block(seqs, left, w_ref, buf_ref.at[lax.rem(i, depth)])
    block_out(t_ref, buf_ref, sem, i).start()

    @pl.when(last())
    def _():
        for n in range(count - depth, count):
            block_out(t_ref, buf_ref, sem, n).wait()


def arrange_kernel(left_ref, couple_ref, rows_ref, w_ref, wide_ref, tall_ref):
    arrange(left_ref, rows_ref, wide_ref)
    widen(couple_ref, w_ref, tall_ref)


def arrange_right(all_ref, rt_ref, right_ref, wide_ref):
    seqs, width, jl = all_ref.shape
    for s in range(seqs):
        for k in range(jl // LANES):
            block = all_ref[s, :, k * LANES : (k + 1) * LANES]
            wide_ref[k, s * width : (s + 1) * width, :] = block.astype(F32)
    for e in range(width):
        for k in range(jl // LANES):
            block = wide_ref.at[k][pl.ds(e, seqs, stride=width), :]
            rt_ref[e * seqs : (e + 1) * seqs, k * LANES : (k + 1) * LANES] = block.astype(BF16)
    for n in range(0, width * seqs, LANES):
        right_ref[:, n : n + LANES] = rt_ref[n : n + LANES, :].astype(F32).T.astype(BF16)


def u_kernel(
    seqs, steps, rows_ref, all_ref, g_ref, w_ref, send_ref, right_ref, u_ref, dl_ref, dw_ref, rt_ref, wide_ref
):
    @pl.when(first())
    def _():
        arrange_right(all_ref, rt_ref, right_ref, wide_ref)
        dw_ref[...] = jnp.zeros_like(dw_ref)

    u_block(seqs, rt_ref, g_ref, u_ref)
    size, width, z = u_ref.shape[0], w_ref.shape[0], g_ref.shape[2]
    start = pl.multiple_of(pl.program_id(0) * size, size)
    dl_ref[pl.ds(start, size), :width] = dot(u_ref[...], w_ref[...], 1, 1)
    left_t = unpack(rows_ref[...], width, steps).T[:width].astype(BF16)
    for n in range(0, u_ref.shape[1], 512):
        dw_ref[:, n : n + 512] += dot(left_t, u_ref[:, n : n + 512])

    @pl.when(last())
    def _():
        share = send_ref.shape[1] - width
        per = width // share
        count = dl_ref.shape[0] // seqs
        for d in range(seqs):
            e, c = d // per, d % per * share
            block = dw_ref[c : c + share, e * z : (e + 1) * z]
            send_ref[d, width:, :] = block.astype(BF16)
            block = dl_ref[pl.ds(d, count, stride=seqs), :].T[:width]
            if count < LANES:
                block = jnp.concatenate([block, jnp.zeros((width, LANES - count), F32)], 1)
            send_ref[d, :width, :] = block.astype(BF16)


def right_kernel(seqs, t_ref, g_ref, out_ref, acc_ref, buf_ref, sem):
    block = stream(t_ref, buf_ref, sem)

    @pl.when(first())
    def _():
        acc_ref[...] = jnp.zeros_like(acc_ref)

    right_block(block, g_ref, acc_ref)

    @pl.when(last())
    def _():
        right_flush(seqs, acc_ref, out_ref)


def pair_kernel(r_ref, bias_ref, t_ref, out_ref, buf_ref, sem):
    pair_block(r_ref, stream(t_ref, buf_ref, sem), bias_ref, out_ref)


def fused_kernel(
    seqs, step, steps, rows_ref, w_ref, r_ref, g_ref, bias_ref, pair_out, out_ref, t_ref, acc_ref
):
    @pl.when(first())
    def _():
        acc_ref[...] = jnp.zeros_like(acc_ref)

    left = unpack(rows_ref[...], w_ref.shape[0], steps)[:, : w_ref.shape[0]].astype(BF16)
    t_block(seqs, left, w_ref, t_ref)
    right_block(t_ref, g_ref, acc_ref)
    pair_block(r_ref, t_ref, bias_ref, pair_out)

    @pl.when(last())
    def _():
        right_flush(seqs, acc_ref, out_ref)


def share_kernel(parts_ref, _, out_ref):
    share = parts_ref.shape[1]
    total = parts_ref[0].astype(F32)
    for d in range(1, parts_ref.shape[0]):
        total += parts_ref[d].astype(F32)
    for d in range(out_ref.shape[0]):
        out_ref[d, :share, :] = total.astype(BF16)


def finish_kernel(rows, cols, left_ref, right_ref, x_ref, w_ref, out_ref, weight_ref):
    width = left_ref.shape[1]
    jl = right_ref.shape[2] - LANES
    il = x_ref.shape[2] // rows
    lefts, rights = [], []
    for r in range(rows):
        terms = [left_ref[r * cols + c].astype(F32) for c in range(cols)]
        lefts.append(sum(terms[1:], terms[0])[:, :il])
    for c in range(cols):
        terms = [right_ref[r * cols + c, :, :jl].astype(F32) for r in range(rows)]
        rights.append(sum(terms[1:], terms[0]))
    both = jnp.concatenate([jnp.concatenate(lefts, 1), jnp.concatenate(rights, 1)], 0)
    grad = dot(w_ref[...], both.astype(BF16))
    xhat, rstd = normalize(x_ref[0].astype(F32))
    mean = jnp.mean(grad, axis=0, keepdims=True)
    proj = jnp.mean(grad * xhat, axis=0, keepdims=True)
    out_ref[0] = (rstd * (grad - mean - xhat * proj)).astype(BF16)
    share = width * width // (rows * cols)
    for d in range(rows * cols):
        e, c = d * share // width, d * share % width
        block = right_ref[d, :share, jl:].astype(F32)
        weight_ref[pl.ds(c * width + e, share, stride=width), :] = block


def on_device(x, split, couple, bias, cot):
    rows, cols = lax.axis_size("row"), lax.axis_size("col")
    seqs = rows * cols
    width = split.shape[1] // 2
    length, depth = x.shape[1], x.shape[2]
    il, jl, z = cot.shape
    part = il * width // LANES
    step = max(2, 512 // seqs)
    steps = part // step
    grid = (il // step,)
    shape = jax.ShapeDtypeStruct
    x_t = x.transpose(0, 2, 1)

    left_send, right_send = call(
        functools.partial(project_kernel, rows, cols),
        (1,),
        [whole(x_t.shape), whole(split.shape)],
        [
            (whole((seqs, part, LANES)), shape((seqs, part, LANES), BF16)),
            (whole((seqs, width, jl)), shape((seqs, width, jl), BF16)),
        ],
        [],
        2 * length * depth * depth,
        (x_t, split),
    )
    left_all = lax.all_to_all(left_send, AXES, 0, 0, tiled=True)
    right_all = lax.all_to_all(right_send, AXES, 0, 0, tiled=True)
    bias_row = bias[None, :]

    unit = 2 * il * jl * z * seqs * width
    small = 2 * il * seqs * width * width * z
    rows_spec = pl.BlockSpec((step * seqs, LANES), lambda i: (lax.rem(i, steps), 0))
    cot_spec = pl.BlockSpec((step, jl, z), lambda i: (i, 0, 0))
    arranged = [
        (whole((part * seqs, LANES)), pltpu.HBM((part * seqs, LANES), BF16)),
        (whole((width, width * z)), pltpu.HBM((width, width * z), BF16)),
    ]
    wides = [pltpu.VMEM((part * seqs, LANES), F32), pltpu.VMEM(couple.shape, F32)]
    t_shape = (il // step, width * seqs, step * z)
    depth = min(DEPTH, t_shape[0])
    any_spec = pl.BlockSpec(memory_space=pl.ANY)
    slots = [pltpu.VMEM((depth, *t_shape[1:]), BF16), pltpu.SemaphoreType.DMA((depth,))]
    stored = 2 * math.prod(t_shape) <= STORED_BYTES
    if stored:
        left_rows, weight, t_all = call(
            functools.partial(t_kernel, seqs, step, steps),
            grid,
            [whole(left_all.shape), whole(couple.shape)],
            arranged + [(any_spec, shape(t_shape, BF16))],
            wides + slots,
            small,
            (left_all, couple),
        )
        right_all, t_all = lax.optimization_barrier((right_all, t_all))
    else:
        left_rows, weight = call(
            arrange_kernel,
            (1,),
            [whole(left_all.shape), whole(couple.shape)],
            arranged,
            wides,
            0,
            (left_all, couple),
        )
    share = width * width // seqs
    left_rows, weight = in_hbm(left_rows), in_hbm(weight)
    right_shape = (jl, width * seqs)
    send_one, right = call(
        functools.partial(u_kernel, seqs, steps),
        grid,
        [rows_spec, whole(right_all.shape), cot_spec, whole(weight.shape)],
        [
            (
                whole((seqs, width + share, LANES)),
                shape((seqs, width + share, LANES), BF16),
            ),
            (whole(right_shape), pltpu.HBM(right_shape, BF16)),
        ],
        [
            pltpu.VMEM((step * seqs, width * z), BF16),
            pltpu.VMEM((il * seqs, LANES), F32),
            pltpu.VMEM((width, width * z), F32),
            pltpu.VMEM((width * seqs, jl), BF16),
            pltpu.VMEM((jl // LANES, width * seqs, LANES), F32),
        ],
        unit + 2 * small,
        (left_rows, right_all, cot, weight),
        limit=U_BYTES,
    )
    got_one = lax.all_to_all(send_one, AXES, 0, 0, tiled=True)
    right_out = (whole((seqs, width, jl)), pltpu.HBM((seqs, width, jl + LANES), BF16))
    acc = pltpu.VMEM((jl // LANES, width * seqs, LANES), F32)
    if stored:
        (right_back,) = call(
            functools.partial(right_kernel, seqs),
            grid,
            [any_spec, cot_spec],
            [right_out],
            [acc] + slots,
            unit,
            (t_all, cot),
        )
        (pair,) = call(
            pair_kernel,
            grid,
            [whole(right.shape), whole(bias_row.shape), any_spec],
            [(cot_spec, shape(cot.shape, BF16))],
            slots,
            unit,
            (right, bias_row, t_all),
        )
    else:
        pair, right_back = call(
            functools.partial(fused_kernel, seqs, step, steps),
            grid,
            [rows_spec, whole(weight.shape), whole(right.shape), cot_spec, whole(bias_row.shape)],
            [(cot_spec, shape(cot.shape, BF16)), right_out],
            [pltpu.VMEM((width * seqs, step * z), BF16), acc],
            2 * unit + small,
            (left_rows, weight, right, cot, bias_row),
        )
    (send_two,) = call(
        share_kernel,
        (1,),
        [
            pl.BlockSpec((seqs, share, LANES), lambda i: (0, width // share, 0)),
            pl.BlockSpec(memory_space=pl.ANY),
        ],
        [
            (
                pl.BlockSpec((seqs, width, LANES), lambda i: (0, 0, jl // LANES)),
                pltpu.HBM(right_back.shape, BF16),
            )
        ],
        [],
        0,
        (got_one, in_hbm(right_back)),
        {1: 0},
        SMALL_BYTES,
    )
    got_two = lax.all_to_all(send_two, AXES, 0, 0, tiled=True)
    align, weight_grad = call(
        functools.partial(finish_kernel, rows, cols),
        (1,),
        [
            pl.BlockSpec((seqs, width, LANES), lambda i: (0, 0, 0)),
            whole(got_two.shape),
            whole(x_t.shape),
            whole(split.shape),
        ],
        [
            (whole(x_t.shape), shape(x_t.shape, BF16)),
            (whole((width * width, z)), shape((width * width, z), F32)),
        ],
        [],
        2 * length * depth * depth,
        (got_one, got_two, x_t, split),
        limit=SMALL_BYTES,
    )
    return pair, align.transpose(0, 2, 1), weight_grad


def solution(mesh):
    placed = (P(AXES, None, None), P(), P(), P(), P("row", "col", None))
    return jax.shard_map(
        on_device,
        mesh=mesh,
        in_specs=placed,
        out_specs=(P("row", "col", None), P(AXES, None, None), P()),
        check_vma=False,
    )
```

```python
import functools
import math

import jax
import jax.numpy as jnp
from jax import lax
from jax.experimental import pallas as pl
from jax.experimental.pallas import tpu as pltpu
from jax.sharding import PartitionSpec as P

F32 = jnp.float32
BF16 = jnp.bfloat16
AXES = ("row", "col")
LANES = 128
VMEM_BYTES = 56 << 20
DEPTH = 3
SMALL_BYTES = 24 << 20
U_BYTES = 48 << 20
STORED_BYTES = 1 << 25


def dot(a, b, da=1, db=0):
    return lax.dot_general(a, b, (((da,), (db,)), ((), ())), preferred_element_type=F32)


def whole(shape):
    return pl.BlockSpec(shape, lambda *_: (0,) * len(shape))


def lanes(blocks):
    return jnp.concatenate(list(blocks), axis=1)


def in_hbm(a):
    return pltpu.with_memory_space_constraint(a, pltpu.HBM)


def call(kernel, grid, ins, outs, scratch, flops, args, aliases={}, limit=VMEM_BYTES):
    nbytes = sum(a.size * a.dtype.itemsize for a in args)
    nbytes += sum(math.prod(o.shape) * o.dtype.itemsize for _, o in outs)
    return pl.pallas_call(
        kernel,
        grid_spec=pltpu.PrefetchScalarGridSpec(
            num_scalar_prefetch=0,
            grid=grid,
            in_specs=ins,
            out_specs=[s for s, _ in outs],
            scratch_shapes=scratch,
        ),
        out_shape=[o for _, o in outs],
        input_output_aliases=aliases,
        compiler_params=pltpu.CompilerParams(vmem_limit_bytes=limit),
        cost_estimate=pl.CostEstimate(flops=flops, bytes_accessed=nbytes, transcendentals=0),
    )(*args)


def normalize(x):
    mu = jnp.mean(x, axis=0, keepdims=True)
    var = jnp.mean((x - mu) * (x - mu), axis=0, keepdims=True)
    rstd = lax.rsqrt(var + 1e-05)
    return (x - mu) * rstd, rstd


def left_kernel(rows, cols, x_ref, w_ref, left_ref):
    xhat, _ = normalize(x_ref[0].astype(F32))
    width = w_ref.shape[1] // 2
    part = left_ref.shape[1]
    groups = LANES // width
    left = dot(xhat.T.astype(BF16), w_ref[:, :width])
    for r in range(rows):
        starts = [(r * groups + k) * part for k in range(groups)]
        packed = lanes(left[n : n + part] for n in starts).astype(BF16)
        for c in range(cols):
            left_ref[r * cols + c] = packed


def project_right_kernel(rows, cols, x_ref, w_ref, right_ref):
    xhat, _ = normalize(x_ref[0].astype(F32))
    width = w_ref.shape[1] // 2
    per_col = right_ref.shape[2]
    right = dot(w_ref[:, width:], xhat.astype(BF16), 0, 0).astype(BF16)
    for r in range(rows):
        for c in range(cols):
            right_ref[r * cols + c] = right[:, c * per_col : (c + 1) * per_col]


def arrange(left_ref, rows_ref, wide_ref):
    seqs, part, _ = left_ref.shape
    for s in range(seqs):
        wide_ref[s * part : (s + 1) * part, :] = left_ref[s].astype(F32)
    for p in range(part):
        block = wide_ref[pl.ds(p, seqs, stride=part), :]
        rows_ref[p * seqs : (p + 1) * seqs, :] = block.astype(BF16)


def unpack(block, width, steps):
    group = pl.program_id(0) // steps
    return pltpu.roll(block.astype(F32), lax.rem(LANES - group * width, LANES), 1)


def t_block(seqs, left, w_ref, t_ref):
    z = t_ref.shape[2]
    for e in range(0, w_ref.shape[1] // z, 2):
        o = (dot(left, w_ref[:, e * z : (e + 2) * z]) * (1.0 / seqs)).astype(BF16)
        for k in range(2):
            for i in range(left.shape[0] // seqs):
                t_ref[i, (e + k) * seqs : (e + k + 1) * seqs, :] = o[
                    i * seqs : (i + 1) * seqs, k * z : (k + 1) * z
                ]


def u_block(seqs, rt_ref, g_ref, u_ref):
    step, _, z = g_ref.shape
    for p in range(0, step, 2):
        pair = jnp.concatenate([g_ref[p], g_ref[p + 1]], axis=1)
        for m in range(0, rt_ref.shape[1], 256):
            right = lanes(rt_ref[k, m : m + 256, :] for k in range(rt_ref.shape[0]))
            o = (dot(right, pair) * (1.0 / seqs)).astype(BF16)
            for k in range(256 // seqs):
                e = m // seqs + k
                for h in range(2):
                    u_ref[e, (p + h) * seqs : (p + h + 1) * seqs, :] = o[
                        k * seqs : (k + 1) * seqs, h * z : (h + 1) * z
                    ]


def pair_block(r_ref, t_ref, bias_ref, out_ref):
    z = out_ref.shape[2]
    for i in range(0, out_ref.shape[0], 2):
        right = lanes(r_ref[n] for n in range(r_ref.shape[0]))
        o = dot(right, lanes((t_ref[i], t_ref[i + 1])))
        for h in range(2):
            out_ref[i + h] = (o[:, h * z : (h + 1) * z] + bias_ref[...].astype(F32)).astype(BF16)


def right_block(t_ref, g_ref, acc_ref):
    grads = jnp.concatenate([g_ref[i] for i in range(g_ref.shape[0])], axis=1)
    for m in range(0, t_ref.shape[1], 256):
        o = dot(lanes(t_ref[i, m : m + 256, :] for i in range(t_ref.shape[0])), grads, 1, 1)
        for k in range(acc_ref.shape[0]):
            acc_ref[k, m : m + 256, :] += o[:, k * LANES : (k + 1) * LANES]


def right_flush(seqs, acc_ref, out_ref):
    for s in range(seqs):
        for k in range(acc_ref.shape[0]):
            block = acc_ref.at[k][pl.ds(s, out_ref.shape[1], stride=seqs), :]
            out_ref[s, :, k * LANES : (k + 1) * LANES] = block.astype(BF16)


def first():
    return pl.program_id(0) == 0


def last():
    return pl.program_id(0) == pl.num_programs(0) - 1


def step_rows(seqs, step, steps, rows_ref, width):
    size = step * seqs
    start = pl.multiple_of(lax.rem(pl.program_id(0), steps) * size, size)
    return unpack(rows_ref[pl.ds(start, size), :], width, steps)[:, :width].astype(BF16)


def widen(couple_ref, w_ref, wide_ref):
    width = w_ref.shape[0]
    z = couple_ref.shape[1]
    wide_ref[...] = couple_ref[...].astype(F32)
    for e in range(couple_ref.shape[0] // width):
        block = wide_ref[pl.ds(e, width, stride=width), :]
        w_ref[:, e * z : (e + 1) * z] = block.astype(BF16)


def block_in(t_ref, buf_ref, sem, n):
    slot = lax.rem(n, buf_ref.shape[0])
    return pltpu.make_async_copy(t_ref.at[n], buf_ref.at[slot], sem.at[slot])


def block_out(t_ref, buf_ref, sem, n):
    slot = lax.rem(n, buf_ref.shape[0])
    return pltpu.make_async_copy(buf_ref.at[slot], t_ref.at[n], sem.at[slot])


def stream(t_ref, buf_ref, sem):
    i, count, depth = pl.program_id(0), t_ref.shape[0], buf_ref.shape[0]

    @pl.when(first())
    def _():
        for n in range(depth - 1):
            block_in(t_ref, buf_ref, sem, n).start()

    @pl.when(i + depth - 1 < count)
    def _():
        block_in(t_ref, buf_ref, sem, i + depth - 1).start()

    block_in(t_ref, buf_ref, sem, i).wait()
    return buf_ref.at[lax.rem(i, depth)]


def t_kernel(
    seqs, step, steps, left_ref, couple_ref, rows_ref, w_ref, t_ref, wide_ref, tall_ref, buf_ref, sem
):
    i, count, depth = pl.program_id(0), t_ref.shape[0], buf_ref.shape[0]

    @pl.when(first())
    def _():
        arrange(left_ref, rows_ref, wide_ref)
        widen(couple_ref, w_ref, tall_ref)

    @pl.when(i >= depth)
    def _():
        block_out(t_ref, buf_ref, sem, i - depth).wait()

    left = step_rows(seqs, step, steps, rows_ref, w_ref.shape[0])
    t_block(seqs, left, w_ref, buf_ref.at[lax.rem(i, depth)])
    block_out(t_ref, buf_ref, sem, i).start()

    @pl.when(last())
    def _():
        for n in range(count - depth, count):
            block_out(t_ref, buf_ref, sem, n).wait()


def arrange_kernel(left_ref, couple_ref, rows_ref, w_ref, wide_ref, tall_ref):
    arrange(left_ref, rows_ref, wide_ref)
    widen(couple_ref, w_ref, tall_ref)


def arrange_right(all_ref, rt_ref, right_ref, wide_ref):
    seqs, width, jl = all_ref.shape
    for s in range(seqs):
        for k in range(jl // LANES):
            block = all_ref[s, :, k * LANES : (k + 1) * LANES]
            wide_ref[k, s * width : (s + 1) * width, :] = block.astype(F32)
    for e in range(width):
        for k in range(jl // LANES):
            block = wide_ref.at[k][pl.ds(e, seqs, stride=width), :]
            rt_ref[k, e * seqs : (e + 1) * seqs, :] = block.astype(BF16)
    for n in range(right_ref.shape[0]):
        for k in range(jl // LANES):
            block = rt_ref[k, n * LANES : (n + 1) * LANES, :].astype(F32).T
            right_ref[n, k * LANES : (k + 1) * LANES, :] = block.astype(BF16)


def u_kernel(
    seqs, steps, rows_ref, all_ref, g_ref, w_ref, send_ref, right_ref, u_ref, dl_ref, dw_ref, rt_ref, wide_ref
):
    @pl.when(first())
    def _():
        arrange_right(all_ref, rt_ref, right_ref, wide_ref)
        dw_ref[...] = jnp.zeros_like(dw_ref)

    u_block(seqs, rt_ref, g_ref, u_ref)
    count, size, z = u_ref.shape
    width = w_ref.shape[0]
    rows = min(size, 256)
    for m in range(0, size, rows):
        start = pl.multiple_of(pl.program_id(0) * size + m, rows)
        block = lanes(u_ref[e, m : m + rows, :] for e in range(count))
        dl_ref[pl.ds(start, rows), :width] = dot(block, w_ref[...], 1, 1)
    left_t = unpack(rows_ref[...], width, steps).T[:width].astype(BF16)
    for e in range(0, count, 4):
        block = lanes(u_ref[e + k] for k in range(4))
        dw_ref[:, e * z : (e + 4) * z] += dot(left_t, block)

    @pl.when(last())
    def _():
        share = send_ref.shape[1] - width
        per = width // share
        count = dl_ref.shape[0] // seqs
        for d in range(seqs):
            e, c = d // per, d % per * share
            block = dw_ref[c : c + share, e * z : (e + 1) * z]
            send_ref[d, width:, :] = block.astype(BF16)
            block = dl_ref[pl.ds(d, count, stride=seqs), :].T[:width]
            if count < LANES:
                block = jnp.concatenate([block, jnp.zeros((width, LANES - count), F32)], 1)
            send_ref[d, :width, :] = block.astype(BF16)


def right_kernel(seqs, t_ref, g_ref, out_ref, acc_ref, buf_ref, sem):
    block = stream(t_ref, buf_ref, sem)

    @pl.when(first())
    def _():
        acc_ref[...] = jnp.zeros_like(acc_ref)

    right_block(block, g_ref, acc_ref)

    @pl.when(last())
    def _():
        right_flush(seqs, acc_ref, out_ref)


def pair_kernel(r_ref, bias_ref, t_ref, out_ref, buf_ref, sem):
    pair_block(r_ref, stream(t_ref, buf_ref, sem), bias_ref, out_ref)


def fused_kernel(
    seqs, step, steps, rows_ref, w_ref, r_ref, g_ref, bias_ref, pair_out, out_ref, t_ref, acc_ref
):
    @pl.when(first())
    def _():
        acc_ref[...] = jnp.zeros_like(acc_ref)

    left = unpack(rows_ref[...], w_ref.shape[0], steps)[:, : w_ref.shape[0]].astype(BF16)
    t_block(seqs, left, w_ref, t_ref)
    right_block(t_ref, g_ref, acc_ref)
    pair_block(r_ref, t_ref, bias_ref, pair_out)

    @pl.when(last())
    def _():
        right_flush(seqs, acc_ref, out_ref)


def share_kernel(parts_ref, _, out_ref):
    share = parts_ref.shape[1]
    total = parts_ref[0].astype(F32)
    for d in range(1, parts_ref.shape[0]):
        total += parts_ref[d].astype(F32)
    for d in range(out_ref.shape[0]):
        out_ref[d, :share, :] = total.astype(BF16)


def finish_kernel(rows, cols, left_ref, right_ref, x_ref, w_ref, out_ref, weight_ref):
    width = left_ref.shape[1]
    jl = right_ref.shape[2] - LANES
    il = x_ref.shape[2] // rows
    lefts, rights = [], []
    for r in range(rows):
        terms = [left_ref[r * cols + c].astype(F32) for c in range(cols)]
        lefts.append(sum(terms[1:], terms[0])[:, :il])
    for c in range(cols):
        terms = [right_ref[r * cols + c, :, :jl].astype(F32) for r in range(rows)]
        rights.append(sum(terms[1:], terms[0]))
    both = jnp.concatenate([jnp.concatenate(lefts, 1), jnp.concatenate(rights, 1)], 0)
    grad = dot(w_ref[...], both.astype(BF16))
    xhat, rstd = normalize(x_ref[0].astype(F32))
    mean = jnp.mean(grad, axis=0, keepdims=True)
    proj = jnp.mean(grad * xhat, axis=0, keepdims=True)
    out_ref[0] = (rstd * (grad - mean - xhat * proj)).astype(BF16)
    share = width * width // (rows * cols)
    for d in range(rows * cols):
        e, c = d * share // width, d * share % width
        block = right_ref[d, :share, jl:].astype(F32)
        weight_ref[pl.ds(c * width + e, share, stride=width), :] = block


def on_device(x, split, couple, bias, cot):
    rows, cols = lax.axis_size("row"), lax.axis_size("col")
    seqs = rows * cols
    width = split.shape[1] // 2
    length, depth = x.shape[1], x.shape[2]
    il, jl, z = cot.shape
    part = il * width // LANES
    step = max(2, 512 // seqs)
    steps = part // step
    grid = (il // step,)
    shape = jax.ShapeDtypeStruct
    x_t = x.transpose(0, 2, 1)

    (left_send,) = call(
        functools.partial(left_kernel, rows, cols),
        (1,),
        [whole(x_t.shape), whole(split.shape)],
        [(whole((seqs, part, LANES)), shape((seqs, part, LANES), BF16))],
        [],
        2 * length * depth * width,
        (x_t, split),
    )
    (right_send,) = call(
        functools.partial(project_right_kernel, rows, cols),
        (1,),
        [whole(x_t.shape), whole(split.shape)],
        [(whole((seqs, width, jl)), shape((seqs, width, jl), BF16))],
        [],
        2 * length * depth * width,
        (x_t, split),
    )
    left_all = lax.all_to_all(left_send, AXES, 0, 0, tiled=True)
    right_all = lax.all_to_all(right_send, AXES, 0, 0, tiled=True)
    bias_row = bias[None, :]

    unit = 2 * il * jl * z * seqs * width
    small = 2 * il * seqs * width * width * z
    rows_spec = pl.BlockSpec((step * seqs, LANES), lambda i: (lax.rem(i, steps), 0))
    cot_spec = pl.BlockSpec((step, jl, z), lambda i: (i, 0, 0))
    arranged = [
        (whole((part * seqs, LANES)), pltpu.HBM((part * seqs, LANES), BF16)),
        (whole((width, width * z)), pltpu.HBM((width, width * z), BF16)),
    ]
    wides = [pltpu.VMEM((part * seqs, LANES), F32), pltpu.VMEM(couple.shape, F32)]
    t_shape = (il // step, step, width * seqs, z)
    depth = min(DEPTH, t_shape[0])
    any_spec = pl.BlockSpec(memory_space=pl.ANY)
    slots = [pltpu.VMEM((depth, *t_shape[1:]), BF16), pltpu.SemaphoreType.DMA((depth,))]
    half = step // 2
    half_depth = min(DEPTH + 1, il // half)
    half_slots = [
        pltpu.VMEM((half_depth, half, *t_shape[2:]), BF16),
        pltpu.SemaphoreType.DMA((half_depth,)),
    ]
    stored = 2 * math.prod(t_shape) <= STORED_BYTES
    if stored:
        left_rows, weight, t_all = call(
            functools.partial(t_kernel, seqs, step, steps),
            grid,
            [whole(left_all.shape), whole(couple.shape)],
            arranged + [(any_spec, shape(t_shape, BF16))],
            wides + slots,
            small,
            (left_all, in_hbm(couple)),
            limit=SMALL_BYTES,
        )
        right_all, t_all = lax.optimization_barrier((right_all, t_all))
    else:
        left_rows, weight = call(
            arrange_kernel,
            (1,),
            [whole(left_all.shape), whole(couple.shape)],
            arranged,
            wides,
            0,
            (left_all, couple),
        )
    share = width * width // seqs
    left_rows, weight = in_hbm(left_rows), in_hbm(weight)
    right_shape = (width * seqs // LANES, jl, LANES)
    send_one, right = call(
        functools.partial(u_kernel, seqs, steps),
        grid,
        [rows_spec, whole(right_all.shape), cot_spec, whole(weight.shape)],
        [
            (
                whole((seqs, width + share, LANES)),
                shape((seqs, width + share, LANES), BF16),
            ),
            (whole(right_shape), pltpu.HBM(right_shape, BF16)),
        ],
        [
            pltpu.VMEM((width, step * seqs, z), BF16),
            pltpu.VMEM((il * seqs, LANES), F32),
            pltpu.VMEM((width, width * z), F32),
            pltpu.VMEM((jl // LANES, width * seqs, LANES), BF16),
            pltpu.VMEM((jl // LANES, width * seqs, LANES), F32),
        ],
        unit + 2 * small,
        (left_rows, right_all, cot, weight),
        limit=U_BYTES,
    )
    got_one = lax.all_to_all(send_one, AXES, 0, 0, tiled=True)
    right_out = (whole((seqs, width, jl)), pltpu.HBM((seqs, width, jl + LANES), BF16))
    acc = pltpu.VMEM((jl // LANES, width * seqs, LANES), F32)
    if stored:
        (right_back,) = call(
            functools.partial(right_kernel, seqs),
            grid,
            [any_spec, cot_spec],
            [right_out],
            [acc] + slots,
            unit,
            (t_all, cot),
        )
        (pair,) = call(
            pair_kernel,
            (il // half,),
            [whole(right.shape), whole(bias_row.shape), any_spec],
            [(pl.BlockSpec((half, jl, z), lambda i: (i, 0, 0)), shape(cot.shape, BF16))],
            half_slots,
            unit,
            (right, bias_row, t_all.reshape(il // half, half, *t_shape[2:])),
        )
    else:
        pair, right_back = call(
            functools.partial(fused_kernel, seqs, step, steps),
            grid,
            [rows_spec, whole(weight.shape), whole(right.shape), cot_spec, whole(bias_row.shape)],
            [(cot_spec, shape(cot.shape, BF16)), right_out],
            [pltpu.VMEM(t_shape[1:], BF16), acc],
            2 * unit + small,
            (left_rows, weight, right, cot, bias_row),
        )
    (send_two,) = call(
        share_kernel,
        (1,),
        [
            pl.BlockSpec((seqs, share, LANES), lambda i: (0, width // share, 0)),
            pl.BlockSpec(memory_space=pl.ANY),
        ],
        [
            (
                pl.BlockSpec((seqs, width, LANES), lambda i: (0, 0, jl // LANES)),
                pltpu.HBM(right_back.shape, BF16),
            )
        ],
        [],
        0,
        (got_one, in_hbm(right_back)),
        {1: 0},
        SMALL_BYTES,
    )
    got_two = lax.all_to_all(send_two, AXES, 0, 0, tiled=True)
    align, weight_grad = call(
        functools.partial(finish_kernel, rows, cols),
        (1,),
        [
            pl.BlockSpec((seqs, width, LANES), lambda i: (0, 0, 0)),
            whole(got_two.shape),
            whole(x_t.shape),
            whole(split.shape),
        ],
        [
            (whole(x_t.shape), shape(x_t.shape, BF16)),
            (whole((width * width, z)), shape((width * width, z), F32)),
        ],
        [],
        2 * length * depth * depth,
        (got_one, got_two, x_t, split),
        limit=SMALL_BYTES,
    )
    return pair, align.transpose(0, 2, 1), weight_grad


def solution(mesh):
    placed = (P(AXES, None, None), P(), P(), P(), P("row", "col", None))
    return jax.shard_map(
        on_device,
        mesh=mesh,
        in_specs=placed,
        out_specs=(P("row", "col", None), P(AXES, None, None), P()),
        check_vma=False,
    )
```
